32 devices in a mesh: section: 4 (over z), row: 2 (over y), col: 4 (over x, core).
Axes of the slice: x: 2, y: 2, z: 4, core: 2. Of those that a mesh axis runs over, the one named last changes fastest.
Arguments:
- tokens: bfloat16 [4, 128, 3072], P('section', 'col', 'row'), may hold values from -6 to 6
- weights: bfloat16 [4, 3072, 12288], P('section', 'row', 'col'), may hold values from -0.109375 to 0.109375
- hidden_grads: bfloat16 [4, 128, 12288], P('section', 'row', 'col'), may hold values from -1.5 to 1.5
Outputs:
- hidden: bfloat16 [4, 128, 12288], P('section', 'row', 'col')
- weight_grad: bfloat16 [4, 3072, 12288], P('section', 'row', 'col')
- passed_grad: bfloat16 [4, 128, 3072], P('section', 'col', 'row')
The draws below stay inside these ranges and needn't reach their ends.
All inputs are finite; a program needn't handle non-finite values.
Results may differ from the reference program's by a relative error of at most 0.0052.
Values may be sent and summed in bfloat16 or wider, within the bound.
No kernel may reach another device: no remote copies, remote signals or barrier semaphores. Data moves between devices by JAX's collectives and lax.ppermute only.
A program may use at most 64 MiB of HBM per device.

```python
import jax
import jax.numpy as jnp
from jax import lax

D = 3072
FF = 12288
TOKENS = 128
SECTIONS = 4
N_ROW = 2


def level_of(key, dims, pieces, low, largest):
    loudness, own = 1.0, jax.random.fold_in(key, 6)
    for axis_at, parts in pieces:
        draws = jnp.exp(jax.random.uniform(jax.random.fold_in(own, axis_at), (parts,), jnp.float32, low / len(pieces), largest / len(pieces)))
        loudness = loudness * jnp.repeat(draws, dims[axis_at] // parts).reshape([-1 if axis == axis_at else 1 for axis in range(len(dims))])
    return loudness


def centred(key, extent, width, bound, split=(), held_as=jnp.bfloat16):
    entries = width * jax.random.normal(key, extent, jnp.float32)
    if split:
        entries = entries * level_of(key, extent, split, -0.22, 0.18)
    return jnp.clip(entries, -bound, bound).astype(held_as)


def setup_inputs(seed: int = 0) -> dict:
    arg_keys = jax.random.split(jax.random.key(seed), 4)
    tokens = centred(arg_keys[0], (SECTIONS, TOKENS, D), 1.0, 6.0, ((0, 4), (1, 4), (2, 2)))
    weights = centred(arg_keys[1], (SECTIONS, D, FF), D ** -0.5, 0.109375, ((0, 4), (1, 2), (2, 4)))
    hidden_grads = centred(arg_keys[2], (SECTIONS, TOKENS, FF), 0.25, 1.5, ((0, 4), (1, 2), (2, 4)))
    return {"tokens": tokens, "weights": weights, "hidden_grads": hidden_grads}


def one_section(section_inputs):
    token_block, weight_block, grad_block = section_inputs
    block_width = D // N_ROW
    running = jnp.zeros((TOKENS, FF), jnp.float32)
    for block_index in range(N_ROW):
        lower = block_index * block_width
        partial_value = jnp.dot(token_block[:, lower:lower + block_width], weight_block[lower:lower + block_width, :], preferred_element_type=jnp.float32)
        partial_value = lax.optimization_barrier(partial_value.astype(jnp.bfloat16)).astype(jnp.float32)
        running = running + partial_value
    hidden = running.astype(jnp.bfloat16)
    weight_grad = jnp.dot(token_block.T, grad_block, preferred_element_type=jnp.float32).astype(jnp.bfloat16)
    input_grad = jnp.dot(grad_block, weight_block.T, preferred_element_type=jnp.float32).astype(jnp.bfloat16)
    return hidden, weight_grad, input_grad


def reference(tokens, weights, hidden_grads):
    hidden, weight_grad, input_grad = lax.map(one_section, (tokens, weights, hidden_grads))
    passed_grad = jnp.concatenate([input_grad[1:], jnp.zeros_like(input_grad[:1])], axis=0)
    return (hidden, weight_grad, passed_grad)
```

```python
import functools

import jax
import jax.numpy as jnp
from jax import lax
from jax.experimental import pallas as pl
from jax.experimental.pallas import tpu as pltpu
from jax.sharding import PartitionSpec as P

F32 = jnp.float32
BF16 = jnp.bfloat16
VMEM = pl.BlockSpec(memory_space=pltpu.VMEM)
MIB = 1 << 20


def shifted(value, axis, steps):
    count = lax.axis_size(axis)
    leading, last = (max(0, -steps), min(count, count - steps))
    return lax.ppermute(value, axis, [(source, source + steps) for source in range(leading, last)])


def swapped(value, axis, distance):
    count = lax.axis_size(axis)
    return lax.ppermute(value, axis, [(source, source ^ distance) for source in range(count)])


def general_step(tokens, weights, hidden_grads):
    token_tile, weight_tile, grad_tile = tokens[0], weights[0], hidden_grads[0]
    tokens_all = lax.all_gather(token_tile, "col", axis=0, tiled=True)
    hidden_sum = lax.psum_scatter(
        jnp.dot(tokens_all, weight_tile, preferred_element_type=F32).astype(BF16),
        "row",
        scatter_dimension=0,
        tiled=True,
    )
    grad_piece = lax.all_gather(grad_tile, "row", axis=0, tiled=True)
    weight_grad = lax.dot_general(
        tokens_all, grad_piece, (((0,), (0,)), ((), ())), preferred_element_type=F32
    ).astype(BF16)
    input_piece = lax.dot_general(
        grad_piece, weight_tile, (((1,), (1,)), ((), ())), preferred_element_type=F32
    )
    input_grad = lax.psum_scatter(input_piece, "col", scatter_dimension=0, tiled=True).astype(BF16)
    return (hidden_sum[None], weight_grad[None], shifted(input_grad, "section", -1)[None])


def call(kernel, out_shapes, args, scratch=(), flops=0, moved=0, name=None, grid=(), in_specs=None, out_specs=None):
    single = not isinstance(out_shapes, (list, tuple))
    shapes = [out_shapes] if single else list(out_shapes)
    in_specs = in_specs or [VMEM] * len(args)
    out_specs = out_specs or [VMEM] * len(shapes)
    result = pl.pallas_call(
        kernel,
        grid=grid,
        out_shape=shapes,
        in_specs=in_specs,
        out_specs=out_specs,
        scratch_shapes=list(scratch),
        compiler_params=pltpu.CompilerParams(vmem_limit_bytes=16 * MIB),
        cost_estimate=pl.CostEstimate(flops=flops, bytes_accessed=moved, transcendentals=0),
        name=name,
    )(*args)
    return result[0] if single else result


def forward_kernel(own, beside, across, diagonal, weight, tokens_out, send_out, keep_out, *, tile):
    rows = own.shape[0]
    row, col = lax.axis_index("row"), lax.axis_index("col")
    chip, core = col // 2, col % 2
    near = jnp.where(chip == row, 2 * rows, 0)
    far = 2 * rows - near
    for ref, start in (
        (own, near + core * rows),
        (beside, near + (1 - core) * rows),
        (across, far + core * rows),
        (diagonal, far + (1 - core) * rows),
    ):
        tokens_out[pl.ds(pl.multiple_of(start, rows), rows), :] = ref[...]
    half = 2 * rows
    for lower in range(0, weight.shape[1], tile):
        product = jnp.dot(
            tokens_out[...], weight[:, lower : lower + tile], preferred_element_type=F32
        ).astype(BF16)
        send_out[:, lower : lower + tile] = product[:half]
        keep_out[:, lower : lower + tile] = product[half:]


def input_grad_kernel(other, own, weight, send_out, keep_out, total, *, tile):
    rows = own.shape[0] // 2
    core = lax.axis_index("col") % 2
    grads = jnp.concatenate([other[...], own[...]], axis=0)
    for lower in range(0, weight.shape[0], tile):
        total[:, lower : lower + tile] = lax.dot_general(
            grads,
            weight[lower : lower + tile, :],
            (((1,), (1,)), ((), ())),
            preferred_element_type=F32,
        )
    for half in range(2):
        mine = pl.multiple_of(2 * half * rows + core * rows, rows)
        theirs = pl.multiple_of(2 * half * rows + (1 - core) * rows, rows)
        keep_out[half * rows : (half + 1) * rows, :] = total[pl.ds(mine, rows), :]
        send_out[half * rows : (half + 1) * rows, :] = total[pl.ds(theirs, rows), :].astype(BF16)


def pair_kernel(keep, received, straight_out, across_out):
    rows = keep.shape[0] // 2
    straight = pl.multiple_of(
        jnp.where(lax.axis_index("col") // 2 == lax.axis_index("row"), rows, 0), rows
    )
    across = pl.multiple_of(rows - straight, rows)
    straight_out[...] = (
        keep[pl.ds(straight, rows), :] + received[pl.ds(straight, rows), :].astype(F32)
    ).astype(BF16)
    across_out[...] = (
        keep[pl.ds(across, rows), :] + received[pl.ds(across, rows), :].astype(F32)
    ).astype(BF16)


def weight_grad_kernel(tokens, other, own, out):
    grads = jnp.concatenate([other[...], own[...]], axis=0)
    out[...] = lax.dot_general(
        tokens[...], grads, (((0,), (0,)), ((), ())), preferred_element_type=F32
    ).astype(BF16)


def paired_step(tokens, weights, hidden_grads):
    own, weight, grads = tokens[0], weights[0], hidden_grads[0]
    rows, width = own.shape
    half, units = grads.shape
    sections = lax.axis_size("section")
    columns = lax.axis_size("col")
    grads_other = swapped(grads, "row", 1)
    across = swapped(own, "col", 2)
    beside = swapped(own, "col", 1)
    diagonal = swapped(across, "col", 1)
    flops = 4 * half * width * units
    tokens_all, hidden_send, hidden_keep = call(
        functools.partial(forward_kernel, tile=512),
        [
            jax.ShapeDtypeStruct((4 * rows, width), BF16),
            jax.ShapeDtypeStruct((half, units), BF16),
            jax.ShapeDtypeStruct((half, units), BF16),
        ],
        (own, beside, across, diagonal, weight),
        flops=flops,
        moved=2 * width * units,
        name="forward",
    )
    hidden_received = swapped(hidden_send, "row", 1)
    piece_send, piece_keep = call(
        functools.partial(input_grad_kernel, tile=256),
        [
            jax.ShapeDtypeStruct((half, width), BF16),
            jax.ShapeDtypeStruct((half, width), F32),
        ],
        (grads_other, grads, weight),
        scratch=[pltpu.VMEM((2 * half, width), F32)],
        flops=flops,
        moved=2 * width * units,
        name="input_grad",
    )
    piece_received = swapped(piece_send, "col", 1)
    straight, crossing = call(
        pair_kernel,
        [jax.ShapeDtypeStruct((rows, width), BF16)] * 2,
        (piece_keep, piece_received),
        moved=8 * half * width,
        name="pair_sum",
    )
    tokens_late, straight, crossing = lax.optimization_barrier((tokens_all, straight, crossing))
    straight_received = shifted(straight, "section", -1)
    crossing_received = lax.ppermute(
        crossing,
        ("section", "col"),
        [
            (section * columns + col, (section - 1) * columns + (col ^ 2))
            for section in range(1, sections)
            for col in range(columns)
        ],
    )
    block = 512
    weight_grad = call(
        weight_grad_kernel,
        jax.ShapeDtypeStruct((width, units), BF16),
        (tokens_late, grads_other, grads),
        grid=(width // block,),
        in_specs=[
            pl.BlockSpec((2 * half, block), lambda step: (0, step)),
            pl.BlockSpec((half, units), lambda step: (0, 0)),
            pl.BlockSpec((half, units), lambda step: (0, 0)),
        ],
        out_specs=[pl.BlockSpec((block, units), lambda step: (step, 0))],
        flops=flops,
        moved=2 * width * units,
        name="weight_grad",
    )
    passed_grad = (straight_received.astype(F32) + crossing_received.astype(F32)).astype(BF16)
    hidden = (hidden_keep.astype(F32) + hidden_received.astype(F32)).astype(BF16)
    return (hidden[None], weight_grad[None], passed_grad[None])


def solution(mesh):
    in_specs = (P("section", "col", "row"), P("section", "row", "col"), P("section", "row", "col"))
    out_specs = (P("section", "row", "col"), P("section", "row", "col"), P("section", "col", "row"))
    paired = mesh.shape["row"] == 2 and mesh.shape["col"] == 4
    return jax.shard_map(
        paired_step if paired else general_step,
        mesh=mesh,
        in_specs=in_specs,
        out_specs=out_specs,
        check_vma=False,
    )
```

```python
import functools

import jax
import jax.numpy as jnp
from jax import lax
from jax.experimental import pallas as pl
from jax.experimental.pallas import tpu as pltpu
from jax.sharding import PartitionSpec as P

F32 = jnp.float32
BF16 = jnp.bfloat16
VMEM = pl.BlockSpec(memory_space=pltpu.VMEM)
MIB = 1 << 20


def shifted(value, axis, steps):
    count = lax.axis_size(axis)
    leading, last = (max(0, -steps), min(count, count - steps))
    return lax.ppermute(value, axis, [(source, source + steps) for source in range(leading, last)])


def swapped(value, axis, distance):
    count = lax.axis_size(axis)
    return lax.ppermute(value, axis, [(source, source ^ distance) for source in range(count)])


def general_step(tokens, weights, hidden_grads):
    token_tile, weight_tile, grad_tile = tokens[0], weights[0], hidden_grads[0]
    tokens_all = lax.all_gather(token_tile, "col", axis=0, tiled=True)
    hidden_sum = lax.psum_scatter(
        jnp.dot(tokens_all, weight_tile, preferred_element_type=F32).astype(BF16),
        "row",
        scatter_dimension=0,
        tiled=True,
    )
    grad_piece = lax.all_gather(grad_tile, "row", axis=0, tiled=True)
    weight_grad = lax.dot_general(
        tokens_all, grad_piece, (((0,), (0,)), ((), ())), preferred_element_type=F32
    ).astype(BF16)
    input_piece = lax.dot_general(
        grad_piece, weight_tile, (((1,), (1,)), ((), ())), preferred_element_type=F32
    )
    input_grad = lax.psum_scatter(input_piece, "col", scatter_dimension=0, tiled=True).astype(BF16)
    return (hidden_sum[None], weight_grad[None], shifted(input_grad, "section", -1)[None])


def call(kernel, out_shapes, args, scratch=(), flops=0, moved=0, name=None, grid=(), in_specs=None, out_specs=None, limit=16 * MIB):
    single = not isinstance(out_shapes, (list, tuple))
    shapes = [out_shapes] if single else list(out_shapes)
    in_specs = in_specs or [VMEM] * len(args)
    out_specs = out_specs or [VMEM] * len(shapes)
    result = pl.pallas_call(
        kernel,
        grid=grid,
        out_shape=shapes,
        in_specs=in_specs,
        out_specs=out_specs,
        scratch_shapes=list(scratch),
        compiler_params=pltpu.CompilerParams(vmem_limit_bytes=limit),
        cost_estimate=pl.CostEstimate(flops=flops, bytes_accessed=moved, transcendentals=0),
        name=name,
    )(*args)
    return result[0] if single else result


def forward_kernel(own, beside, across, diagonal, weight, tokens_out, send_out, keep_out, *, tile):
    rows = own.shape[0]
    row, col = lax.axis_index("row"), lax.axis_index("col")
    chip, core = col // 2, col % 2
    near = jnp.where(chip == row, 2 * rows, 0)
    far = 2 * rows - near
    for ref, start in (
        (own, near + core * rows),
        (beside, near + (1 - core) * rows),
        (across, far + core * rows),
        (diagonal, far + (1 - core) * rows),
    ):
        tokens_out[pl.ds(pl.multiple_of(start, rows), rows), :] = ref[...]
    half = 2 * rows
    for lower in range(0, weight.shape[1], tile):
        product = jnp.dot(
            tokens_out[...], weight[:, lower : lower + tile], preferred_element_type=F32
        ).astype(BF16)
        send_out[:, lower : lower + tile] = product[:half]
        keep_out[:, lower : lower + tile] = product[half:]


def load_kernel(weight, own, grads, weight_out, own_out, grads_out, sems):
    copies = [
        pltpu.make_async_copy(source, target, sems.at[index])
        for index, (source, target) in enumerate(
            ((own, own_out), (grads, grads_out), (weight, weight_out))
        )
    ]
    for copy in copies:
        copy.start()
    for copy in copies:
        copy.wait()


def input_grad_kernel(other, own, weight, send_out, keep_out, *, tile):
    rows = own.shape[0] // 2
    core = lax.axis_index("col") % 2
    mine = pl.multiple_of(core * rows, rows)
    theirs = pl.multiple_of((1 - core) * rows, rows)
    grads = jnp.concatenate(
        [ref[pl.ds(start, rows), :] for start in (theirs, mine) for ref in (other, own)], axis=0
    ).T
    for lower in range(0, weight.shape[0], tile):
        total = jnp.dot(
            weight[lower : lower + tile, :], grads, preferred_element_type=F32
        ).T
        send_out[:, lower : lower + tile] = total[: 2 * rows].astype(BF16)
        keep_out[:, lower : lower + tile] = total[2 * rows :]


def pair_kernel(keep, received, straight_out, across_out):
    rows = keep.shape[0] // 2
    straight = pl.multiple_of(
        jnp.where(lax.axis_index("col") // 2 == lax.axis_index("row"), rows, 0), rows
    )
    across = pl.multiple_of(rows - straight, rows)
    straight_out[...] = (
        keep[pl.ds(straight, rows), :] + received[pl.ds(straight, rows), :].astype(F32)
    ).astype(BF16)
    across_out[...] = (
        keep[pl.ds(across, rows), :] + received[pl.ds(across, rows), :].astype(F32)
    ).astype(BF16)


def weight_grad_kernel(tokens, other, own, out, turned, blocks, sems, *, tile):
    turned[...] = tokens[...].T
    copies = []
    for index in range(out.shape[1] // tile):
        lower = index * tile
        grads = jnp.concatenate(
            [other[:, lower : lower + tile], own[:, lower : lower + tile]], axis=0
        )
        blocks[index] = jnp.dot(turned[...], grads, preferred_element_type=F32).astype(BF16)
        copy = pltpu.make_async_copy(
            blocks.at[index], out.at[:, pl.ds(lower, tile)], sems.at[index]
        )
        copy.start()
        copies.append(copy)
    for copy in copies:
        copy.wait()


def sum_kernel(hidden_keep, hidden_received, straight, crossing, hidden_out, passed_out):
    hidden_out[...] = (hidden_keep[...].astype(F32) + hidden_received[...].astype(F32)).astype(BF16)
    passed_out[...] = (straight[...].astype(F32) + crossing[...].astype(F32)).astype(BF16)


def paired_step(tokens, weights, hidden_grads):
    own, weight, grads = tokens[0], weights[0], hidden_grads[0]
    rows, width = own.shape
    half, units = grads.shape
    sections = lax.axis_size("section")
    columns = lax.axis_size("col")
    grads_other = swapped(grads, "row", 1)
    across = swapped(own, "col", 2)
    beside = swapped(own, "col", 1)
    flops = 4 * half * width * units
    anywhere = pl.BlockSpec(memory_space=pltpu.HBM)
    weight, own, grads = call(
        load_kernel,
        [jax.ShapeDtypeStruct(value.shape, BF16) for value in (weight, own, grads)],
        [pltpu.with_memory_space_constraint(value, pltpu.HBM) for value in (weight, own, grads)],
        scratch=[pltpu.SemaphoreType.DMA((3,))],
        in_specs=[anywhere] * 3,
        moved=4 * width * units,
        limit=40 * MIB,
        name="load",
    )
    across, weight = lax.optimization_barrier((across, weight))
    diagonal = swapped(across, "col", 1)
    tokens_all, hidden_send, hidden_keep = call(
        functools.partial(forward_kernel, tile=512),
        [
            jax.ShapeDtypeStruct((4 * rows, width), BF16),
            jax.ShapeDtypeStruct((half, units), BF16),
            jax.ShapeDtypeStruct((half, units), BF16),
        ],
        (own, beside, across, diagonal, weight),
        flops=flops,
        moved=2 * width * units,
        name="forward",
    )
    hidden_received = swapped(hidden_send, "row", 1)
    piece_send, piece_keep = call(
        functools.partial(input_grad_kernel, tile=256),
        [
            jax.ShapeDtypeStruct((half, width), BF16),
            jax.ShapeDtypeStruct((half, width), F32),
        ],
        (grads_other, grads, weight),
        flops=flops,
        moved=2 * width * units,
        name="input_grad",
    )
    piece_received = swapped(piece_send, "col", 1)
    straight, crossing = call(
        pair_kernel,
        [jax.ShapeDtypeStruct((rows, width), BF16)] * 2,
        (piece_keep, piece_received),
        moved=8 * half * width,
        name="pair_sum",
    )
    tokens_late, straight, crossing = lax.optimization_barrier((tokens_all, straight, crossing))
    straight_received = shifted(straight, "section", -1)
    crossing_received = lax.ppermute(
        crossing,
        ("section", "col"),
        [
            (section * columns + col, (section - 1) * columns + (col ^ 2))
            for section in range(1, sections)
            for col in range(columns)
        ],
    )
    block = 512
    weight_grad = call(
        functools.partial(weight_grad_kernel, tile=block),
        jax.ShapeDtypeStruct((width, units), BF16),
        (tokens_late, grads_other, grads),
        scratch=[
            pltpu.VMEM((width, 2 * half), BF16),
            pltpu.VMEM((units // block, width, block), BF16),
            pltpu.SemaphoreType.DMA((units // block,)),
        ],
        out_specs=[anywhere],
        flops=flops,
        moved=2 * width * units,
        name="weight_grad",
    )
    hidden, passed_grad = call(
        sum_kernel,
        [jax.ShapeDtypeStruct((half, units), BF16), jax.ShapeDtypeStruct((rows, width), BF16)],
        (hidden_keep, hidden_received, straight_received, crossing_received),
        moved=8 * half * units,
        name="final_sum",
    )
    return (hidden[None], weight_grad[None], passed_grad[None])


def solution(mesh):
    in_specs = (P("section", "col", "row"), P("section", "row", "col"), P("section", "row", "col"))
    out_specs = (P("section", "row", "col"), P("section", "row", "col"), P("section", "col", "row"))
    paired = mesh.shape["row"] == 2 and mesh.shape["col"] == 4
    return jax.shard_map(
        paired_step if paired else general_step,
        mesh=mesh,
        in_specs=in_specs,
        out_specs=out_specs,
        check_vma=False,
    )
```

```python
import functools

import jax
import jax.numpy as jnp
from jax import lax
from jax.experimental import pallas as pl
from jax.experimental.pallas import tpu as pltpu
from jax.sharding import PartitionSpec as P

F32 = jnp.float32
BF16 = jnp.bfloat16
VMEM = pl.BlockSpec(memory_space=pltpu.VMEM)
MIB = 1 << 20


def shifted(value, axis, steps):
    count = lax.axis_size(axis)
    leading, last = (max(0, -steps), min(count, count - steps))
    return lax.ppermute(value, axis, [(source, source + steps) for source in range(leading, last)])


def swapped(value, axis, distance):
    count = lax.axis_size(axis)
    return lax.ppermute(value, axis, [(source, source ^ distance) for source in range(count)])


def general_step(tokens, weights, hidden_grads):
    token_tile, weight_tile, grad_tile = tokens[0], weights[0], hidden_grads[0]
    tokens_all = lax.all_gather(token_tile, "col", axis=0, tiled=True)
    hidden_sum = lax.psum_scatter(
        jnp.dot(tokens_all, weight_tile, preferred_element_type=F32).astype(BF16),
        "row",
        scatter_dimension=0,
        tiled=True,
    )
    grad_piece = lax.all_gather(grad_tile, "row", axis=0, tiled=True)
    weight_grad = lax.dot_general(
        tokens_all, grad_piece, (((0,), (0,)), ((), ())), preferred_element_type=F32
    ).astype(BF16)
    input_piece = lax.dot_general(
        grad_piece, weight_tile, (((1,), (1,)), ((), ())), preferred_element_type=F32
    )
    input_grad = lax.psum_scatter(input_piece, "col", scatter_dimension=0, tiled=True).astype(BF16)
    return (hidden_sum[None], weight_grad[None], shifted(input_grad, "section", -1)[None])


def call(kernel, out_shapes, args, scratch=(), flops=0, moved=0, name=None, grid=(), in_specs=None, out_specs=None, limit=16 * MIB):
    single = not isinstance(out_shapes, (list, tuple))
    shapes = [out_shapes] if single else list(out_shapes)
    in_specs = in_specs or [VMEM] * len(args)
    out_specs = out_specs or [VMEM] * len(shapes)
    result = pl.pallas_call(
        kernel,
        grid=grid,
        out_shape=shapes,
        in_specs=in_specs,
        out_specs=out_specs,
        scratch_shapes=list(scratch),
        compiler_params=pltpu.CompilerParams(vmem_limit_bytes=limit),
        cost_estimate=pl.CostEstimate(flops=flops, bytes_accessed=moved, transcendentals=0),
        name=name,
    )(*args)
    return result[0] if single else result


def forward_kernel(own, beside, across, diagonal, weight, tokens_out, send_out, keep_out, *, tile):
    rows = own.shape[0]
    row, col = lax.axis_index("row"), lax.axis_index("col")
    chip, core = col // 2, col % 2
    near = jnp.where(chip == row, 2 * rows, 0)
    far = 2 * rows - near
    for ref, start in (
        (own, near + core * rows),
        (beside, near + (1 - core) * rows),
        (across, far + core * rows),
        (diagonal, far + (1 - core) * rows),
    ):
        tokens_out[pl.ds(pl.multiple_of(start, rows), rows), :] = ref[...]
    half = 2 * rows
    for lower in range(0, weight.shape[1], tile):
        product = jnp.dot(
            tokens_out[...], weight[:, lower : lower + tile], preferred_element_type=F32
        ).astype(BF16)
        send_out[:, lower : lower + tile] = product[:half]
        keep_out[:, lower : lower + tile] = product[half:]


def turn(weight, out, lower, upper, offset):
    size = min(256, weight.shape[1])
    down = lax.broadcasted_iota(jnp.int32, (size, size), 0)
    right = lax.broadcasted_iota(jnp.int32, (size, size), 1)
    identity = jnp.where(down == right, 1.0, 0.0).astype(BF16)
    for unit in range(0, weight.shape[1], size):
        out[unit : unit + size, lower - offset : upper - offset] = lax.dot_general(
            identity,
            weight[lower:upper, unit : unit + size],
            (((1,), (1,)), ((), ())),
            preferred_element_type=F32,
        ).astype(BF16)


def load_kernel(weight, own, grads, weight_out, turned_out, own_out, grads_out, sems, *, chunk):
    small = [
        pltpu.make_async_copy(own, own_out, sems.at[0]),
        pltpu.make_async_copy(grads, grads_out, sems.at[1]),
    ]
    large = [
        pltpu.make_async_copy(
            weight.at[pl.ds(lower, chunk)], weight_out.at[pl.ds(lower, chunk)], sems.at[2 + index]
        )
        for index, lower in enumerate(range(0, weight.shape[0], chunk))
    ]
    for copy in large[:1] + small + large[1:]:
        copy.start()
    for index, copy in enumerate(large):
        copy.wait()
        if (index + 1) * chunk <= turned_out.shape[1]:
            turn(weight_out, turned_out, index * chunk, (index + 1) * chunk, 0)
    for copy in small:
        copy.wait()


def turn_kernel(weight, out, *, chunk):
    done = weight.shape[0] - out.shape[1]
    for lower in range(done, weight.shape[0], chunk):
        turn(weight, out, lower, lower + chunk, done)


def input_grad_kernel(other, own, first, second, send_out, keep_out, *, tile):
    rows = own.shape[0] // 2
    core = lax.axis_index("col") % 2
    mine = pl.multiple_of(core * rows, rows)
    theirs = pl.multiple_of((1 - core) * rows, rows)
    grads = jnp.concatenate(
        [ref[pl.ds(start, rows), :] for start in (theirs, mine) for ref in (other, own)], axis=0
    )
    offset = 0
    for turned in (first, second):
        for lower in range(0, turned.shape[1], tile):
            total = jnp.dot(grads, turned[:, lower : lower + tile], preferred_element_type=F32)
            columns = pl.ds(offset + lower, tile)
            send_out[:, columns] = total[: 2 * rows].astype(BF16)
            keep_out[:, columns] = total[2 * rows :]
        offset += turned.shape[1]


def pair_kernel(keep, received, straight_out, across_out):
    rows = keep.shape[0] // 2
    straight = pl.multiple_of(
        jnp.where(lax.axis_index("col") // 2 == lax.axis_index("row"), rows, 0), rows
    )
    across = pl.multiple_of(rows - straight, rows)
    straight_out[...] = (
        keep[pl.ds(straight, rows), :] + received[pl.ds(straight, rows), :].astype(F32)
    ).astype(BF16)
    across_out[...] = (
        keep[pl.ds(across, rows), :] + received[pl.ds(across, rows), :].astype(F32)
    ).astype(BF16)


def weight_grad_kernel(tokens, other, own, out, turned, blocks, sems, *, tile):
    turned[...] = tokens[...].T
    copies = []
    for index in range(out.shape[1] // tile):
        lower = index * tile
        grads = jnp.concatenate(
            [other[:, lower : lower + tile], own[:, lower : lower + tile]], axis=0
        )
        blocks[index] = jnp.dot(turned[...], grads, preferred_element_type=F32).astype(BF16)
        copy = pltpu.make_async_copy(
            blocks.at[index], out.at[:, pl.ds(lower, tile)], sems.at[index]
        )
        copy.start()
        copies.append(copy)
    for copy in copies:
        copy.wait()


def sum_kernel(hidden_keep, hidden_received, straight, crossing, hidden_out, passed_out):
    hidden_out[...] = (hidden_keep[...].astype(F32) + hidden_received[...].astype(F32)).astype(BF16)
    passed_out[...] = (straight[...].astype(F32) + crossing[...].astype(F32)).astype(BF16)


def paired_step(tokens, weights, hidden_grads):
    own, weight, grads = tokens[0], weights[0], hidden_grads[0]
    rows, width = own.shape
    half, units = grads.shape
    sections = lax.axis_size("section")
    columns = lax.axis_size("col")
    grads_other = swapped(grads, "row", 1)
    across = swapped(own, "col", 2)
    beside = swapped(own, "col", 1)
    flops = 4 * half * width * units
    anywhere = pl.BlockSpec(memory_space=pltpu.HBM)
    chunk = 256
    early = chunk * 4
    weight, turned_first, own, grads = call(
        functools.partial(load_kernel, chunk=chunk),
        [
            jax.ShapeDtypeStruct(shape, BF16)
            for shape in (weight.shape, (units, early), own.shape, grads.shape)
        ],
        [pltpu.with_memory_space_constraint(value, pltpu.HBM) for value in (weight, own, grads)],
        scratch=[pltpu.SemaphoreType.DMA((2 + width // chunk,))],
        in_specs=[anywhere] * 3,
        moved=4 * width * units,
        limit=16 * MIB,
        name="load",
    )
    across, weight = lax.optimization_barrier((across, weight))
    diagonal = swapped(across, "col", 1)
    turned_second = call(
        functools.partial(turn_kernel, chunk=chunk),
        jax.ShapeDtypeStruct((units, width - early), BF16),
        (weight,),
        flops=2 * units * (width - early) * chunk,
        moved=4 * units * (width - early),
        name="turn",
    )
    diagonal, turned_second = lax.optimization_barrier((diagonal, turned_second))
    tokens_all, hidden_send, hidden_keep = call(
        functools.partial(forward_kernel, tile=512),
        [
            jax.ShapeDtypeStruct((4 * rows, width), BF16),
            jax.ShapeDtypeStruct((half, units), BF16),
            jax.ShapeDtypeStruct((half, units), BF16),
        ],
        (own, beside, across, diagonal, weight),
        flops=flops,
        moved=2 * width * units,
        name="forward",
    )
    hidden_received = swapped(hidden_send, "row", 1)
    piece_send, piece_keep = call(
        functools.partial(input_grad_kernel, tile=256),
        [
            jax.ShapeDtypeStruct((half, width), BF16),
            jax.ShapeDtypeStruct((half, width), F32),
        ],
        (grads_other, grads, turned_first, turned_second),
        flops=flops,
        moved=2 * width * units,
        name="input_grad",
    )
    piece_received = swapped(piece_send, "col", 1)
    straight, crossing = call(
        pair_kernel,
        [jax.ShapeDtypeStruct((rows, width), BF16)] * 2,
        (piece_keep, piece_received),
        moved=8 * half * width,
        name="pair_sum",
    )
    tokens_late, straight, crossing = lax.optimization_barrier((tokens_all, straight, crossing))
    straight_received = shifted(straight, "section", -1)
    crossing_received = lax.ppermute(
        crossing,
        ("section", "col"),
        [
            (section * columns + col, (section - 1) * columns + (col ^ 2))
            for section in range(1, sections)
            for col in range(columns)
        ],
    )
    block = 512
    weight_grad = call(
        functools.partial(weight_grad_kernel, tile=block),
        jax.ShapeDtypeStruct((width, units), BF16),
        (tokens_late, grads_other, grads),
        scratch=[
            pltpu.VMEM((width, 2 * half), BF16),
            pltpu.VMEM((units // block, width, block), BF16),
            pltpu.SemaphoreType.DMA((units // block,)),
        ],
        out_specs=[anywhere],
        flops=flops,
        moved=2 * width * units,
        name="weight_grad",
    )
    hidden, passed_grad = call(
        sum_kernel,
        [jax.ShapeDtypeStruct((half, units), BF16), jax.ShapeDtypeStruct((rows, width), BF16)],
        (hidden_keep, hidden_received, straight_received, crossing_received),
        moved=8 * half * units,
        name="final_sum",
    )
    return (hidden[None], weight_grad[None], passed_grad[None])


def solution(mesh):
    in_specs = (P("section", "col", "row"), P("section", "row", "col"), P("section", "row", "col"))
    out_specs = (P("section", "row", "col"), P("section", "row", "col"), P("section", "col", "row"))
    paired = mesh.shape["row"] == 2 and mesh.shape["col"] == 4
    return jax.shard_map(
        paired_step if paired else general_step,
        mesh=mesh,
        in_specs=in_specs,
        out_specs=out_specs,
        check_vma=False,
    )
```

```python
import functools

import jax
import jax.numpy as jnp
from jax import lax
from jax.experimental import pallas as pl
from jax.experimental.pallas import tpu as pltpu
from jax.sharding import PartitionSpec as P

F32 = jnp.float32
BF16 = jnp.bfloat16
VMEM = pl.BlockSpec(memory_space=pltpu.VMEM)
MIB = 1 << 20


def shifted(value, axis, steps):
    count = lax.axis_size(axis)
    leading, last = (max(0, -steps), min(count, count - steps))
    return lax.ppermute(value, axis, [(source, source + steps) for source in range(leading, last)])


def paired_sections(value, first, crossing):
    sections, columns = lax.axis_size("section"), lax.axis_size("col")
    pairs = []
    for section in range(sections):
        partner = section + 1 if (section - first) % 2 == 0 else section - 1
        for col in range(columns):
            if 0 <= partner < sections:
                target = (partner, col ^ 2 if crossing else col)
            else:
                target = (section, col ^ 1)
            pairs.append((section * columns + col, target[0] * columns + target[1]))
    return lax.ppermute(value, ("section", "col"), pairs)


def swapped(value, axis, distance):
    count = lax.axis_size(axis)
    return lax.ppermute(value, axis, [(source, source ^ distance) for source in range(count)])


def general_step(tokens, weights, hidden_grads):
    token_tile, weight_tile, grad_tile = tokens[0], weights[0], hidden_grads[0]
    tokens_all = lax.all_gather(token_tile, "col", axis=0, tiled=True)
    hidden_sum = lax.psum_scatter(
        jnp.dot(tokens_all, weight_tile, preferred_element_type=F32).astype(BF16),
        "row",
        scatter_dimension=0,
        tiled=True,
    )
    grad_piece = lax.all_gather(grad_tile, "row", axis=0, tiled=True)
    weight_grad = lax.dot_general(
        tokens_all, grad_piece, (((0,), (0,)), ((), ())), preferred_element_type=F32
    ).astype(BF16)
    input_piece = lax.dot_general(
        grad_piece, weight_tile, (((1,), (1,)), ((), ())), preferred_element_type=F32
    )
    input_grad = lax.psum_scatter(input_piece, "col", scatter_dimension=0, tiled=True).astype(BF16)
    return (hidden_sum[None], weight_grad[None], shifted(input_grad, "section", -1)[None])


def call(kernel, out_shapes, args, scratch=(), flops=0, moved=0, name=None, grid=(), in_specs=None, out_specs=None, limit=16 * MIB):
    single = not isinstance(out_shapes, (list, tuple))
    shapes = [out_shapes] if single else list(out_shapes)
    in_specs = in_specs or [VMEM] * len(args)
    out_specs = out_specs or [VMEM] * len(shapes)
    result = pl.pallas_call(
        kernel,
        grid=grid,
        out_shape=shapes,
        in_specs=in_specs,
        out_specs=out_specs,
        scratch_shapes=list(scratch),
        compiler_params=pltpu.CompilerParams(vmem_limit_bytes=limit),
        cost_estimate=pl.CostEstimate(flops=flops, bytes_accessed=moved, transcendentals=0),
        name=name,
    )(*args)
    return result[0] if single else result


def forward_kernel(own, beside, across, diagonal, weight, tokens_out, send_out, keep_out, *, tile):
    rows = own.shape[0]
    row, col = lax.axis_index("row"), lax.axis_index("col")
    chip, core = col // 2, col % 2
    near = jnp.where(chip == row, 2 * rows, 0)
    far = 2 * rows - near
    for ref, start in (
        (own, near + core * rows),
        (beside, near + (1 - core) * rows),
        (across, far + core * rows),
        (diagonal, far + (1 - core) * rows),
    ):
        tokens_out[pl.ds(pl.multiple_of(start, rows), rows), :] = ref[...]
    half = 2 * rows
    for lower in range(0, weight.shape[1], tile):
        product = jnp.dot(
            tokens_out[...], weight[:, lower : lower + tile], preferred_element_type=F32
        ).astype(BF16)
        send_out[:, lower : lower + tile] = product[:half]
        keep_out[:, lower : lower + tile] = product[half:]


def turn(weight, out, lower, upper, offset):
    size = min(256, weight.shape[1])
    down = lax.broadcasted_iota(jnp.int32, (size, size), 0)
    right = lax.broadcasted_iota(jnp.int32, (size, size), 1)
    identity = jnp.where(down == right, 1.0, 0.0).astype(BF16)
    for unit in range(0, weight.shape[1], size):
        out[unit : unit + size, lower - offset : upper - offset] = lax.dot_general(
            identity,
            weight[lower:upper, unit : unit + size],
            (((1,), (1,)), ((), ())),
            preferred_element_type=F32,
        ).astype(BF16)


def load_kernel(weight, own, grads, weight_out, turned_out, own_out, grads_out, sems, *, chunk):
    small = [
        pltpu.make_async_copy(own, own_out, sems.at[0]),
        pltpu.make_async_copy(grads, grads_out, sems.at[1]),
    ]
    large = [
        pltpu.make_async_copy(
            weight.at[pl.ds(lower, chunk)], weight_out.at[pl.ds(lower, chunk)], sems.at[2 + index]
        )
        for index, lower in enumerate(range(0, weight.shape[0], chunk))
    ]
    for copy in large[:1] + small + large[1:]:
        copy.start()
    for index, copy in enumerate(large):
        copy.wait()
        if (index + 1) * chunk <= turned_out.shape[1]:
            turn(weight_out, turned_out, index * chunk, (index + 1) * chunk, 0)
    for copy in small:
        copy.wait()


def turn_kernel(weight, out, *, chunk):
    done = weight.shape[0] - out.shape[1]
    for lower in range(done, weight.shape[0], chunk):
        turn(weight, out, lower, lower + chunk, done)


def input_grad_kernel(other, own, first, second, send_out, keep_out, *, tile):
    rows = own.shape[0] // 2
    core = lax.axis_index("col") % 2
    mine = pl.multiple_of(core * rows, rows)
    theirs = pl.multiple_of((1 - core) * rows, rows)
    grads = jnp.concatenate(
        [ref[pl.ds(start, rows), :] for start in (theirs, mine) for ref in (other, own)], axis=0
    )
    offset = 0
    for turned in (first, second):
        for lower in range(0, turned.shape[1], tile):
            total = jnp.dot(grads, turned[:, lower : lower + tile], preferred_element_type=F32)
            columns = pl.ds(offset + lower, tile)
            send_out[:, columns] = total[: 2 * rows].astype(BF16)
            keep_out[:, columns] = total[2 * rows :]
        offset += turned.shape[1]


def pair_kernel(keep, received, *outs):
    rows = keep.shape[0] // 2
    matches = lax.axis_index("col") // 2 == lax.axis_index("row")
    straight = pl.multiple_of(jnp.where(matches, rows, 0), rows)
    crossing = pl.multiple_of(rows - straight, rows)
    for index, start in enumerate((crossing, straight)):
        total = (
            keep[pl.ds(start, rows), :] + received[pl.ds(start, rows), :].astype(F32)
        ).astype(BF16)
        for out in outs[index::2]:
            out[...] = total


def weight_grad_kernel(tokens, other, own, out, turned, blocks, sems, *, tile):
    turned[...] = tokens[...].T
    copies = []
    for index in range(out.shape[1] // tile):
        lower = index * tile
        grads = jnp.concatenate(
            [other[:, lower : lower + tile], own[:, lower : lower + tile]], axis=0
        )
        blocks[index] = jnp.dot(turned[...], grads, preferred_element_type=F32).astype(BF16)
        copy = pltpu.make_async_copy(
            blocks.at[index], out.at[:, pl.ds(lower, tile)], sems.at[index]
        )
        copy.start()
        copies.append(copy)
    for copy in copies:
        copy.wait()


def sum_kernel(hidden_keep, hidden_received, *refs):
    *received, hidden_out, passed_out = refs
    hidden_out[...] = (hidden_keep[...].astype(F32) + hidden_received[...].astype(F32)).astype(BF16)
    sums = [
        received[index][...].astype(F32) + received[index + 1][...].astype(F32)
        for index in (0, 2)
    ]
    section = lax.axis_index("section")
    last = section == lax.axis_size("section") - 1
    passed = jnp.where(section % 2 == 0, sums[0], sums[1])
    passed_out[...] = jnp.where(last, jnp.zeros_like(passed), passed).astype(BF16)


def paired_step(tokens, weights, hidden_grads):
    own, weight, grads = tokens[0], weights[0], hidden_grads[0]
    rows, width = own.shape
    half, units = grads.shape
    grads_other = swapped(grads, "row", 1)
    across = swapped(own, "col", 2)
    beside = swapped(own, "col", 1)
    flops = 4 * half * width * units
    anywhere = pl.BlockSpec(memory_space=pltpu.HBM)
    chunk = 256
    early = chunk * 4
    weight, turned_first, own, grads = call(
        functools.partial(load_kernel, chunk=chunk),
        [
            jax.ShapeDtypeStruct(shape, BF16)
            for shape in (weight.shape, (units, early), own.shape, grads.shape)
        ],
        [pltpu.with_memory_space_constraint(value, pltpu.HBM) for value in (weight, own, grads)],
        scratch=[pltpu.SemaphoreType.DMA((2 + width // chunk,))],
        in_specs=[anywhere] * 3,
        moved=4 * width * units,
        limit=16 * MIB,
        name="load",
    )
    across, weight = lax.optimization_barrier((across, weight))
    diagonal = swapped(across, "col", 1)
    turned_second = call(
        functools.partial(turn_kernel, chunk=chunk),
        jax.ShapeDtypeStruct((units, width - early), BF16),
        (weight,),
        flops=2 * units * (width - early) * chunk,
        moved=4 * units * (width - early),
        name="turn",
    )
    diagonal, turned_second = lax.optimization_barrier((diagonal, turned_second))
    tokens_all, hidden_send, hidden_keep = call(
        functools.partial(forward_kernel, tile=512),
        [
            jax.ShapeDtypeStruct((4 * rows, width), BF16),
            jax.ShapeDtypeStruct((half, units), BF16),
            jax.ShapeDtypeStruct((half, units), BF16),
        ],
        (own, beside, across, diagonal, weight),
        flops=flops,
        moved=2 * width * units,
        name="forward",
    )
    hidden_received = swapped(hidden_send, "row", 1)
    piece_send, piece_keep = call(
        functools.partial(input_grad_kernel, tile=256),
        [
            jax.ShapeDtypeStruct((half, width), BF16),
            jax.ShapeDtypeStruct((half, width), F32),
        ],
        (grads_other, grads, turned_first, turned_second),
        flops=flops,
        moved=2 * width * units,
        name="input_grad",
    )
    piece_received = swapped(piece_send, "col", 1)
    pieces = call(
        pair_kernel,
        [jax.ShapeDtypeStruct((rows, width), BF16)] * 4,
        (piece_keep, piece_received),
        moved=8 * half * width,
        name="pair_sum",
    )
    tokens_late, *pieces = lax.optimization_barrier((tokens_all, *pieces))
    received = [
        paired_sections(piece, index // 2, index % 2 == 0) for index, piece in enumerate(pieces)
    ]
    block = 512
    weight_grad = call(
        functools.partial(weight_grad_kernel, tile=block),
        jax.ShapeDtypeStruct((width, units), BF16),
        (tokens_late, grads_other, grads),
        scratch=[
            pltpu.VMEM((width, 2 * half), BF16),
            pltpu.VMEM((units // block, width, block), BF16),
            pltpu.SemaphoreType.DMA((units // block,)),
        ],
        out_specs=[anywhere],
        flops=flops,
        moved=2 * width * units,
        name="weight_grad",
    )
    hidden, passed_grad = call(
        sum_kernel,
        [jax.ShapeDtypeStruct((half, units), BF16), jax.ShapeDtypeStruct((rows, width), BF16)],
        [hidden_keep, hidden_received] + received,
        moved=8 * half * units,
        name="final_sum",
    )
    return (hidden[None], weight_grad[None], passed_grad[None])


def solution(mesh):
    in_specs = (P("section", "col", "row"), P("section", "row", "col"), P("section", "row", "col"))
    out_specs = (P("section", "row", "col"), P("section", "row", "col"), P("section", "col", "row"))
    paired = mesh.shape["row"] == 2 and mesh.shape["col"] == 4
    return jax.shard_map(
        paired_step if paired else general_step,
        mesh=mesh,
        in_specs=in_specs,
        out_specs=out_specs,
        check_vma=False,
    )
```

```python
import functools

import jax
import jax.numpy as jnp
from jax import lax
from jax.experimental import pallas as pl
from jax.experimental.pallas import tpu as pltpu
from jax.sharding import PartitionSpec as P

F32 = jnp.float32
BF16 = jnp.bfloat16
VMEM = pl.BlockSpec(memory_space=pltpu.VMEM)
MIB = 1 << 20


def shifted(value, axis, steps):
    count = lax.axis_size(axis)
    leading, last = (max(0, -steps), min(count, count - steps))
    return lax.ppermute(value, axis, [(source, source + steps) for source in range(leading, last)])


def paired_sections(value, first, crossing):
    sections, columns = lax.axis_size("section"), lax.axis_size("col")
    pairs = []
    for section in range(sections):
        partner = section + 1 if (section - first) % 2 == 0 else section - 1
        for col in range(columns):
            if 0 <= partner < sections:
                target = (partner, col ^ 2 if crossing else col)
            else:
                target = (section, col ^ 1)
            pairs.append((section * columns + col, target[0] * columns + target[1]))
    return lax.ppermute(value, ("section", "col"), pairs)


def swapped(value, axis, distance):
    count = lax.axis_size(axis)
    return lax.ppermute(value, axis, [(source, source ^ distance) for source in range(count)])


def general_step(tokens, weights, hidden_grads):
    token_tile, weight_tile, grad_tile = tokens[0], weights[0], hidden_grads[0]
    tokens_all = lax.all_gather(token_tile, "col", axis=0, tiled=True)
    hidden_sum = lax.psum_scatter(
        jnp.dot(tokens_all, weight_tile, preferred_element_type=F32).astype(BF16),
        "row",
        scatter_dimension=0,
        tiled=True,
    )
    grad_piece = lax.all_gather(grad_tile, "row", axis=0, tiled=True)
    weight_grad = lax.dot_general(
        tokens_all, grad_piece, (((0,), (0,)), ((), ())), preferred_element_type=F32
    ).astype(BF16)
    input_piece = lax.dot_general(
        grad_piece, weight_tile, (((1,), (1,)), ((), ())), preferred_element_type=F32
    )
    input_grad = lax.psum_scatter(input_piece, "col", scatter_dimension=0, tiled=True).astype(BF16)
    return (hidden_sum[None], weight_grad[None], shifted(input_grad, "section", -1)[None])


def call(kernel, out_shapes, args, scratch=(), flops=0, moved=0, name=None, grid=(), in_specs=None, out_specs=None, limit=16 * MIB, aliases={}):
    single = not isinstance(out_shapes, (list, tuple))
    shapes = [out_shapes] if single else list(out_shapes)
    in_specs = in_specs or [VMEM] * len(args)
    out_specs = out_specs or [VMEM] * len(shapes)
    result = pl.pallas_call(
        kernel,
        grid=grid,
        out_shape=shapes,
        in_specs=in_specs,
        out_specs=out_specs,
        scratch_shapes=list(scratch),
        input_output_aliases=aliases,
        compiler_params=pltpu.CompilerParams(vmem_limit_bytes=limit),
        cost_estimate=pl.CostEstimate(flops=flops, bytes_accessed=moved, transcendentals=0),
        name=name,
    )(*args)
    return result[0] if single else result


def forward_kernel(own, beside, across, diagonal, weight, tokens_out, send_out, keep_out, *, tile):
    rows = own.shape[0]
    row, col = lax.axis_index("row"), lax.axis_index("col")
    chip, core = col // 2, col % 2
    near = jnp.where(chip == row, 2 * rows, 0)
    far = 2 * rows - near
    for ref, start in (
        (own, near + core * rows),
        (beside, near + (1 - core) * rows),
        (across, far + core * rows),
        (diagonal, far + (1 - core) * rows),
    ):
        tokens_out[pl.ds(pl.multiple_of(start, rows), rows), :] = ref[...]
    half = 2 * rows
    for lower in range(0, weight.shape[1], tile):
        product = jnp.dot(
            tokens_out[...], weight[:, lower : lower + tile], preferred_element_type=F32
        ).astype(BF16)
        send_out[:, lower : lower + tile] = product[:half]
        keep_out[:, lower : lower + tile] = product[half:]


def turn(weight, out, lower, upper, offset):
    size = min(256, weight.shape[1])
    down = lax.broadcasted_iota(jnp.int32, (size, size), 0)
    right = lax.broadcasted_iota(jnp.int32, (size, size), 1)
    identity = jnp.where(down == right, 1.0, 0.0).astype(BF16)
    for unit in range(0, weight.shape[1], size):
        out[unit : unit + size, lower - offset : upper - offset] = lax.dot_general(
            identity,
            weight[lower:upper, unit : unit + size],
            (((1,), (1,)), ((), ())),
            preferred_element_type=F32,
        ).astype(BF16)


def load_kernel(weight, own, grads, weight_out, turned_out, own_out, grads_out, sems, *, chunk):
    small = [
        pltpu.make_async_copy(own, own_out, sems.at[0]),
        pltpu.make_async_copy(grads, grads_out, sems.at[1]),
    ]
    large = [
        pltpu.make_async_copy(
            weight.at[pl.ds(lower, chunk)], weight_out.at[pl.ds(lower, chunk)], sems.at[2 + index]
        )
        for index, lower in enumerate(range(0, weight.shape[0], chunk))
    ]
    for copy in large[:1] + small + large[1:]:
        copy.start()
    for index, copy in enumerate(large):
        copy.wait()
        if (index + 1) * chunk <= turned_out.shape[1]:
            turn(weight_out, turned_out, index * chunk, (index + 1) * chunk, 0)
    for copy in small:
        copy.wait()


def turn_kernel(weight, out, *, chunk):
    done = weight.shape[0] - out.shape[1]
    for lower in range(done, weight.shape[0], chunk):
        turn(weight, out, lower, lower + chunk, done)


def input_grad_kernel(other, own, first, second, send_out, keep_out, *, tile):
    rows = own.shape[0] // 2
    core = lax.axis_index("col") % 2
    mine = pl.multiple_of(core * rows, rows)
    theirs = pl.multiple_of((1 - core) * rows, rows)
    grads = jnp.concatenate(
        [ref[pl.ds(start, rows), :] for start in (theirs, mine) for ref in (other, own)], axis=0
    )
    offset = 0
    for turned in (first, second):
        for lower in range(0, turned.shape[1], tile):
            total = jnp.dot(grads, turned[:, lower : lower + tile], preferred_element_type=F32)
            columns = pl.ds(offset + lower, tile)
            send_out[:, columns] = total[: 2 * rows].astype(BF16)
            keep_out[:, columns] = total[2 * rows :]
        offset += turned.shape[1]


def pair_kernel(keep, received, *outs):
    rows = keep.shape[0] // 2
    matches = lax.axis_index("col") // 2 == lax.axis_index("row")
    straight = pl.multiple_of(jnp.where(matches, rows, 0), rows)
    crossing = pl.multiple_of(rows - straight, rows)
    for index, start in enumerate((crossing, straight)):
        total = (
            keep[pl.ds(start, rows), :] + received[pl.ds(start, rows), :].astype(F32)
        ).astype(BF16)
        for out in outs[index::2]:
            out[...] = total


def weight_grad_kernel(tokens, other, own, out, turned, blocks, sems, *, tile):
    turned[...] = tokens[...].T
    copies = []
    for index in range(out.shape[1] // tile):
        lower = index * tile
        grads = jnp.concatenate(
            [other[:, lower : lower + tile], own[:, lower : lower + tile]], axis=0
        )
        blocks[index] = jnp.dot(turned[...], grads, preferred_element_type=F32).astype(BF16)
        rows = out.shape[0] // 2
        for part in range(2):
            copy = pltpu.make_async_copy(
                blocks.at[index, pl.ds(part * rows, rows)],
                out.at[pl.ds(part * rows, rows), pl.ds(lower, tile)],
                sems.at[2 * index + part],
            )
            copy.start(priority=part)
            copies.append(copy)
    for copy in copies:
        copy.wait()


def sum_kernel(hidden_keep, hidden_received, *refs):
    *received, hidden_out, passed_out, hidden_held, passed_held, sems = refs
    copies = []
    rows = hidden_keep.shape[0] // 2
    for index in range(2):
        part = pl.ds(index * rows, rows)
        hidden_held[part, :] = (
            hidden_keep[part, :].astype(F32) + hidden_received[part, :].astype(F32)
        ).astype(BF16)
        copies.append(
            pltpu.make_async_copy(hidden_held.at[part], hidden_out.at[part], sems.at[index])
        )
        copies[-1].start()
    sums = [
        received[index][...].astype(F32) + received[index + 1][...].astype(F32)
        for index in (0, 2)
    ]
    section = lax.axis_index("section")
    last = section == lax.axis_size("section") - 1
    passed = jnp.where(section % 2 == 0, sums[0], sums[1])
    passed_held[...] = jnp.where(last, jnp.zeros_like(passed), passed).astype(BF16)
    copies.append(pltpu.make_async_copy(passed_held, passed_out, sems.at[2]))
    copies[-1].start()
    for copy in copies:
        copy.wait()


def paired_step(tokens, weights, hidden_grads):
    own, weight, grads = tokens[0], weights[0], hidden_grads[0]
    rows, width = own.shape
    half, units = grads.shape
    grads_other = swapped(grads, "row", 1)
    across = swapped(own, "col", 2)
    beside = swapped(own, "col", 1)
    flops = 4 * half * width * units
    anywhere = pl.BlockSpec(memory_space=pltpu.HBM)
    chunk = 256
    early = chunk * 4
    weight, turned_first, own, grads = call(
        functools.partial(load_kernel, chunk=chunk),
        [
            jax.ShapeDtypeStruct(shape, BF16)
            for shape in (weight.shape, (units, early), own.shape, grads.shape)
        ],
        [pltpu.with_memory_space_constraint(value, pltpu.HBM) for value in (weight, own, grads)],
        scratch=[pltpu.SemaphoreType.DMA((2 + width // chunk,))],
        in_specs=[anywhere] * 3,
        moved=4 * width * units,
        limit=16 * MIB,
        name="load",
    )
    across, weight = lax.optimization_barrier((across, weight))
    diagonal = swapped(across, "col", 1)
    turned_second = call(
        functools.partial(turn_kernel, chunk=chunk),
        jax.ShapeDtypeStruct((units, width - early), BF16),
        (weight,),
        flops=2 * units * (width - early) * chunk,
        moved=4 * units * (width - early),
        name="turn",
    )
    diagonal, turned_second = lax.optimization_barrier((diagonal, turned_second))
    tokens_all, hidden_send, hidden_keep = call(
        functools.partial(forward_kernel, tile=512),
        [
            jax.ShapeDtypeStruct((4 * rows, width), BF16),
            jax.ShapeDtypeStruct((half, units), BF16),
            jax.ShapeDtypeStruct((half, units), BF16),
        ],
        (own, beside, across, diagonal, weight),
        flops=flops,
        moved=2 * width * units,
        name="forward",
    )
    hidden_received = swapped(hidden_send, "row", 1)
    piece_send, piece_keep = call(
        functools.partial(input_grad_kernel, tile=256),
        [
            jax.ShapeDtypeStruct((half, width), BF16),
            jax.ShapeDtypeStruct((half, width), F32),
        ],
        (grads_other, grads, turned_first, turned_second),
        flops=flops,
        moved=2 * width * units,
        name="input_grad",
    )
    piece_received = swapped(piece_send, "col", 1)
    pieces = call(
        pair_kernel,
        [jax.ShapeDtypeStruct((rows, width), BF16)] * 4,
        (piece_keep, piece_received),
        moved=8 * half * width,
        name="pair_sum",
    )
    tokens_late, *pieces = lax.optimization_barrier((tokens_all, *pieces))
    received = [
        paired_sections(piece, index // 2, index % 2 == 0) for index, piece in enumerate(pieces)
    ]
    block = 512
    weight_grad = call(
        functools.partial(weight_grad_kernel, tile=block),
        jax.ShapeDtypeStruct((width, units), BF16),
        (tokens_late, grads_other, grads),
        scratch=[
            pltpu.VMEM((width, 2 * half), BF16),
            pltpu.VMEM((units // block, width, block), BF16),
            pltpu.SemaphoreType.DMA((2 * units // block,)),
        ],
        out_specs=[anywhere],
        flops=flops,
        moved=2 * width * units,
        name="weight_grad",
    )
    hidden, passed_grad = call(
        sum_kernel,
        [jax.ShapeDtypeStruct((half, units), BF16), jax.ShapeDtypeStruct((rows, width), BF16)],
        [hidden_keep, hidden_received] + received,
        scratch=[
            pltpu.VMEM((half, units), BF16),
            pltpu.VMEM((rows, width), BF16),
            pltpu.SemaphoreType.DMA((3,)),
        ],
        out_specs=[anywhere] * 2,
        moved=8 * half * units,
        name="final_sum",
    )
    return (hidden[None], weight_grad[None], passed_grad[None])


def solution(mesh):
    in_specs = (P("section", "col", "row"), P("section", "row", "col"), P("section", "row", "col"))
    out_specs = (P("section", "row", "col"), P("section", "row", "col"), P("section", "col", "row"))
    paired = mesh.shape["row"] == 2 and mesh.shape["col"] == 4
    return jax.shard_map(
        paired_step if paired else general_step,
        mesh=mesh,
        in_specs=in_specs,
        out_specs=out_specs,
        check_vma=False,
    )
```

```python
import functools

import jax
import jax.numpy as jnp
from jax import lax
from jax.experimental import pallas as pl
from jax.experimental.pallas import tpu as pltpu
from jax.sharding import PartitionSpec as P

F32 = jnp.float32
BF16 = jnp.bfloat16
VMEM = pl.BlockSpec(memory_space=pltpu.VMEM)
MIB = 1 << 20


def shifted(value, axis, steps):
    count = lax.axis_size(axis)
    leading, last = (max(0, -steps), min(count, count - steps))
    return lax.ppermute(value, axis, [(source, source + steps) for source in range(leading, last)])


def paired_sections(value, first, crossing):
    sections, columns = lax.axis_size("section"), lax.axis_size("col")
    pairs = []
    for section in range(sections):
        partner = section + 1 if (section - first) % 2 == 0 else section - 1
        for col in range(columns):
            if 0 <= partner < sections:
                target = (partner, col ^ 2 if crossing else col)
            else:
                target = (section, col ^ 1)
            pairs.append((section * columns + col, target[0] * columns + target[1]))
    return lax.ppermute(value, ("section", "col"), pairs)


def swapped(value, axis, distance):
    count = lax.axis_size(axis)
    return lax.ppermute(value, axis, [(source, source ^ distance) for source in range(count)])


def general_step(tokens, weights, hidden_grads):
    token_tile, weight_tile, grad_tile = tokens[0], weights[0], hidden_grads[0]
    tokens_all = lax.all_gather(token_tile, "col", axis=0, tiled=True)
    hidden_sum = lax.psum_scatter(
        jnp.dot(tokens_all, weight_tile, preferred_element_type=F32).astype(BF16),
        "row",
        scatter_dimension=0,
        tiled=True,
    )
    grad_piece = lax.all_gather(grad_tile, "row", axis=0, tiled=True)
    weight_grad = lax.dot_general(
        tokens_all, grad_piece, (((0,), (0,)), ((), ())), preferred_element_type=F32
    ).astype(BF16)
    input_piece = lax.dot_general(
        grad_piece, weight_tile, (((1,), (1,)), ((), ())), preferred_element_type=F32
    )
    input_grad = lax.psum_scatter(input_piece, "col", scatter_dimension=0, tiled=True).astype(BF16)
    return (hidden_sum[None], weight_grad[None], shifted(input_grad, "section", -1)[None])


def call(kernel, out_shapes, args, scratch=(), flops=0, moved=0, name=None, grid=(), in_specs=None, out_specs=None, limit=16 * MIB, aliases={}):
    single = not isinstance(out_shapes, (list, tuple))
    shapes = [out_shapes] if single else list(out_shapes)
    in_specs = in_specs or [VMEM] * len(args)
    out_specs = out_specs or [VMEM] * len(shapes)
    result = pl.pallas_call(
        kernel,
        grid=grid,
        out_shape=shapes,
        in_specs=in_specs,
        out_specs=out_specs,
        scratch_shapes=list(scratch),
        input_output_aliases=aliases,
        compiler_params=pltpu.CompilerParams(vmem_limit_bytes=limit),
        cost_estimate=pl.CostEstimate(flops=flops, bytes_accessed=moved, transcendentals=0),
        name=name,
    )(*args)
    return result[0] if single else result


def forward_kernel(own, beside, across, diagonal, weight, tokens_out, send_out, keep_out, *, tile):
    rows = own.shape[0]
    row, col = lax.axis_index("row"), lax.axis_index("col")
    chip, core = col // 2, col % 2
    near = jnp.where(chip == row, 2 * rows, 0)
    far = 2 * rows - near
    for ref, start in (
        (own, near + core * rows),
        (beside, near + (1 - core) * rows),
        (across, far + core * rows),
        (diagonal, far + (1 - core) * rows),
    ):
        tokens_out[pl.ds(pl.multiple_of(start, rows), rows), :] = ref[...]
    half = 2 * rows
    for lower in range(0, weight.shape[1], tile):
        product = jnp.dot(
            tokens_out[...], weight[:, lower : lower + tile], preferred_element_type=F32
        ).astype(BF16)
        send_out[:, lower : lower + tile] = product[:half]
        keep_out[:, lower : lower + tile] = product[half:]


def turn(weight, out, lower, upper, offset):
    size = min(256, weight.shape[1])
    down = lax.broadcasted_iota(jnp.int32, (size, size), 0)
    right = lax.broadcasted_iota(jnp.int32, (size, size), 1)
    identity = jnp.where(down == right, 1.0, 0.0).astype(BF16)
    for unit in range(0, weight.shape[1], size):
        out[unit : unit + size, lower - offset : upper - offset] = lax.dot_general(
            identity,
            weight[lower:upper, unit : unit + size],
            (((1,), (1,)), ((), ())),
            preferred_element_type=F32,
        ).astype(BF16)


def load_kernel(weight, own, grads, weight_out, turned_out, own_out, grads_out, sems, *, chunk):
    small = [
        pltpu.make_async_copy(own, own_out, sems.at[0]),
        pltpu.make_async_copy(grads, grads_out, sems.at[1]),
    ]
    large = [
        pltpu.make_async_copy(
            weight.at[pl.ds(lower, chunk)], weight_out.at[pl.ds(lower, chunk)], sems.at[2 + index]
        )
        for index, lower in enumerate(range(0, weight.shape[0], chunk))
    ]
    for copy in large[:1] + small + large[1:]:
        copy.start()
    for index, copy in enumerate(large):
        copy.wait()
        if (index + 1) * chunk <= turned_out.shape[1]:
            turn(weight_out, turned_out, index * chunk, (index + 1) * chunk, 0)
    for copy in small:
        copy.wait()


def turn_kernel(weight, out, *, chunk):
    done = weight.shape[0] - out.shape[1]
    for lower in range(done, weight.shape[0], chunk):
        turn(weight, out, lower, lower + chunk, done)


def input_grad_kernel(other, own, first, second, send_out, keep_out, *, tile):
    rows = own.shape[0] // 2
    core = lax.axis_index("col") % 2
    mine = pl.multiple_of(core * rows, rows)
    theirs = pl.multiple_of((1 - core) * rows, rows)
    grads = jnp.concatenate(
        [ref[pl.ds(start, rows), :] for start in (theirs, mine) for ref in (other, own)], axis=0
    )
    offset = 0
    for turned in (first, second):
        for lower in range(0, turned.shape[1], tile):
            total = jnp.dot(grads, turned[:, lower : lower + tile], preferred_element_type=F32)
            columns = pl.ds(offset + lower, tile)
            send_out[:, columns] = total[: 2 * rows].astype(BF16)
            keep_out[:, columns] = total[2 * rows :]
        offset += turned.shape[1]


def pair_kernel(keep, received, *outs):
    rows = keep.shape[0] // 2
    matches = lax.axis_index("col") // 2 == lax.axis_index("row")
    straight = pl.multiple_of(jnp.where(matches, rows, 0), rows)
    crossing = pl.multiple_of(rows - straight, rows)
    for index, start in enumerate((crossing, straight)):
        total = (
            keep[pl.ds(start, rows), :] + received[pl.ds(start, rows), :].astype(F32)
        ).astype(BF16)
        for out in outs[index::2]:
            out[...] = total


def weight_grad_kernel(tokens, other, own, out, turned, blocks, sems, *, tile):
    turned[...] = tokens[...].T
    copies = []
    for index in range(out.shape[1] // tile):
        lower = index * tile
        grads = jnp.concatenate(
            [other[:, lower : lower + tile], own[:, lower : lower + tile]], axis=0
        )
        blocks[index] = jnp.dot(turned[...], grads, preferred_element_type=F32).astype(BF16)
        rows = out.shape[0] // 2
        for part in range(2):
            copy = pltpu.make_async_copy(
                blocks.at[index, pl.ds(part * rows, rows)],
                out.at[pl.ds(part * rows, rows), pl.ds(lower, tile)],
                sems.at[2 * index + part],
            )
            copy.start(priority=part)
            copies.append(copy)
    for copy in copies:
        copy.wait()


def hidden_kernel(keep, received, out):
    out[...] = (keep[...].astype(F32) + received[...].astype(F32)).astype(BF16)


def sum_kernel(hidden, *refs):
    *received, hidden_out, passed_out, passed_held, sems = refs
    copies = [pltpu.make_async_copy(hidden, hidden_out, sems.at[0])]
    copies[0].start()
    sums = [
        received[index][...].astype(F32) + received[index + 1][...].astype(F32)
        for index in (0, 2)
    ]
    section = lax.axis_index("section")
    last = section == lax.axis_size("section") - 1
    passed = jnp.where(section % 2 == 0, sums[0], sums[1])
    passed_held[...] = jnp.where(last, jnp.zeros_like(passed), passed).astype(BF16)
    copies.append(pltpu.make_async_copy(passed_held, passed_out, sems.at[1]))
    copies[-1].start()
    for copy in copies:
        copy.wait()


def paired_step(tokens, weights, hidden_grads):
    own, weight, grads = tokens[0], weights[0], hidden_grads[0]
    rows, width = own.shape
    half, units = grads.shape
    grads_other = swapped(grads, "row", 1)
    across = swapped(own, "col", 2)
    beside = swapped(own, "col", 1)
    flops = 4 * half * width * units
    anywhere = pl.BlockSpec(memory_space=pltpu.HBM)
    chunk = 256
    early = chunk * 4
    weight, turned_first, own, grads = call(
        functools.partial(load_kernel, chunk=chunk),
        [
            jax.ShapeDtypeStruct(shape, BF16)
            for shape in (weight.shape, (units, early), own.shape, grads.shape)
        ],
        [pltpu.with_memory_space_constraint(value, pltpu.HBM) for value in (weight, own, grads)],
        scratch=[pltpu.SemaphoreType.DMA((2 + width // chunk,))],
        in_specs=[anywhere] * 3,
        moved=4 * width * units,
        limit=16 * MIB,
        name="load",
    )
    across, weight = lax.optimization_barrier((across, weight))
    diagonal = swapped(across, "col", 1)
    turned_second = call(
        functools.partial(turn_kernel, chunk=chunk),
        jax.ShapeDtypeStruct((units, width - early), BF16),
        (weight,),
        flops=2 * units * (width - early) * chunk,
        moved=4 * units * (width - early),
        name="turn",
    )
    diagonal, turned_second = lax.optimization_barrier((diagonal, turned_second))
    tokens_all, hidden_send, hidden_keep = call(
        functools.partial(forward_kernel, tile=512),
        [
            jax.ShapeDtypeStruct((4 * rows, width), BF16),
            jax.ShapeDtypeStruct((half, units), BF16),
            jax.ShapeDtypeStruct((half, units), BF16),
        ],
        (own, beside, across, diagonal, weight),
        flops=flops,
        moved=2 * width * units,
        name="forward",
    )
    hidden_received = swapped(hidden_send, "row", 1)
    piece_send, piece_keep = call(
        functools.partial(input_grad_kernel, tile=256),
        [
            jax.ShapeDtypeStruct((half, width), BF16),
            jax.ShapeDtypeStruct((half, width), F32),
        ],
        (grads_other, grads, turned_first, turned_second),
        flops=flops,
        moved=2 * width * units,
        name="input_grad",
    )
    piece_received = swapped(piece_send, "col", 1)
    pieces = call(
        pair_kernel,
        [jax.ShapeDtypeStruct((rows, width), BF16)] * 4,
        (piece_keep, piece_received),
        moved=8 * half * width,
        name="pair_sum",
    )
    tokens_late, *pieces = lax.optimization_barrier((tokens_all, *pieces))
    received = [
        paired_sections(piece, index // 2, index % 2 == 0) for index, piece in enumerate(pieces)
    ]
    block = 512
    weight_grad = call(
        functools.partial(weight_grad_kernel, tile=block),
        jax.ShapeDtypeStruct((width, units), BF16),
        (tokens_late, grads_other, grads),
        scratch=[
            pltpu.VMEM((width, 2 * half), BF16),
            pltpu.VMEM((units // block, width, block), BF16),
            pltpu.SemaphoreType.DMA((2 * units // block,)),
        ],
        out_specs=[anywhere],
        flops=flops,
        moved=2 * width * units,
        name="weight_grad",
    )
    hidden_received, weight_grad = lax.optimization_barrier((hidden_received, weight_grad))
    hidden = call(
        hidden_kernel,
        jax.ShapeDtypeStruct((half, units), BF16),
        (hidden_keep, hidden_received),
        moved=6 * half * units,
        name="hidden_sum",
    )
    hidden, passed_grad = call(
        sum_kernel,
        [jax.ShapeDtypeStruct((half, units), BF16), jax.ShapeDtypeStruct((rows, width), BF16)],
        [hidden] + received,
        scratch=[
            pltpu.VMEM((rows, width), BF16),
            pltpu.SemaphoreType.DMA((2,)),
        ],
        out_specs=[anywhere] * 2,
        moved=8 * half * units,
        name="final_sum",
    )
    return (hidden[None], weight_grad[None], passed_grad[None])


def solution(mesh):
    in_specs = (P("section", "col", "row"), P("section", "row", "col"), P("section", "row", "col"))
    out_specs = (P("section", "row", "col"), P("section", "row", "col"), P("section", "col", "row"))
    paired = mesh.shape["row"] == 2 and mesh.shape["col"] == 4
    return jax.shard_map(
        paired_step if paired else general_step,
        mesh=mesh,
        in_specs=in_specs,
        out_specs=out_specs,
        check_vma=False,
    )
```

```python
import functools

import jax
import jax.numpy as jnp
from jax import lax
from jax.experimental import pallas as pl
from jax.experimental.pallas import tpu as pltpu
from jax.sharding import PartitionSpec as P

F32 = jnp.float32
BF16 = jnp.bfloat16
VMEM = pl.BlockSpec(memory_space=pltpu.VMEM)
MIB = 1 << 20


def shifted(value, axis, steps):
    count = lax.axis_size(axis)
    leading, last = (max(0, -steps), min(count, count - steps))
    return lax.ppermute(value, axis, [(source, source + steps) for source in range(leading, last)])


def paired_sections(value, first, crossing):
    sections, columns = lax.axis_size("section"), lax.axis_size("col")
    pairs = []
    for section in range(sections):
        partner = section + 1 if (section - first) % 2 == 0 else section - 1
        for col in range(columns):
            if 0 <= partner < sections:
                target = (partner, col ^ 2 if crossing else col)
            else:
                target = (section, col ^ 1)
            pairs.append((section * columns + col, target[0] * columns + target[1]))
    return lax.ppermute(value, ("section", "col"), pairs)


def swapped(value, axis, distance):
    count = lax.axis_size(axis)
    return lax.ppermute(value, axis, [(source, source ^ distance) for source in range(count)])


def general_step(tokens, weights, hidden_grads):
    token_tile, weight_tile, grad_tile = tokens[0], weights[0], hidden_grads[0]
    tokens_all = lax.all_gather(token_tile, "col", axis=0, tiled=True)
    hidden_sum = lax.psum_scatter(
        jnp.dot(tokens_all, weight_tile, preferred_element_type=F32).astype(BF16),
        "row",
        scatter_dimension=0,
        tiled=True,
    )
    grad_piece = lax.all_gather(grad_tile, "row", axis=0, tiled=True)
    weight_grad = lax.dot_general(
        tokens_all, grad_piece, (((0,), (0,)), ((), ())), preferred_element_type=F32
    ).astype(BF16)
    input_piece = lax.dot_general(
        grad_piece, weight_tile, (((1,), (1,)), ((), ())), preferred_element_type=F32
    )
    input_grad = lax.psum_scatter(input_piece, "col", scatter_dimension=0, tiled=True).astype(BF16)
    return (hidden_sum[None], weight_grad[None], shifted(input_grad, "section", -1)[None])


def call(kernel, out_shapes, args, scratch=(), flops=0, moved=0, name=None, grid=(), in_specs=None, out_specs=None, limit=16 * MIB, aliases={}):
    single = not isinstance(out_shapes, (list, tuple))
    shapes = [out_shapes] if single else list(out_shapes)
    in_specs = in_specs or [VMEM] * len(args)
    out_specs = out_specs or [VMEM] * len(shapes)
    result = pl.pallas_call(
        kernel,
        grid=grid,
        out_shape=shapes,
        in_specs=in_specs,
        out_specs=out_specs,
        scratch_shapes=list(scratch),
        input_output_aliases=aliases,
        compiler_params=pltpu.CompilerParams(vmem_limit_bytes=limit),
        cost_estimate=pl.CostEstimate(flops=flops, bytes_accessed=moved, transcendentals=0),
        name=name,
    )(*args)
    return result[0] if single else result


def forward_kernel(own, beside, across, diagonal, weight, tokens_out, send_out, keep_out, *, tile):
    rows = own.shape[0]
    row, col = lax.axis_index("row"), lax.axis_index("col")
    chip, core = col // 2, col % 2
    near = jnp.where(chip == row, 2 * rows, 0)
    far = 2 * rows - near
    for ref, start in (
        (own, near + core * rows),
        (beside, near + (1 - core) * rows),
        (across, far + core * rows),
        (diagonal, far + (1 - core) * rows),
    ):
        tokens_out[pl.ds(pl.multiple_of(start, rows), rows), :] = ref[...]
    half = 2 * rows
    for lower in range(0, weight.shape[1], tile):
        product = jnp.dot(
            tokens_out[...], weight[:, lower : lower + tile], preferred_element_type=F32
        ).astype(BF16)
        send_out[:, lower : lower + tile] = product[:half]
        keep_out[:, lower : lower + tile] = product[half:]


def turn(weight, out, lower, upper, offset):
    size = min(256, weight.shape[1])
    down = lax.broadcasted_iota(jnp.int32, (size, size), 0)
    right = lax.broadcasted_iota(jnp.int32, (size, size), 1)
    identity = jnp.where(down == right, 1.0, 0.0).astype(BF16)
    for unit in range(0, weight.shape[1], size):
        out[unit : unit + size, lower - offset : upper - offset] = lax.dot_general(
            identity,
            weight[lower:upper, unit : unit + size],
            (((1,), (1,)), ((), ())),
            preferred_element_type=F32,
        ).astype(BF16)


def load_kernel(weight, own, grads, weight_out, turned_out, own_out, grads_out, sems, *, chunk):
    small = [
        pltpu.make_async_copy(own, own_out, sems.at[0]),
        pltpu.make_async_copy(grads, grads_out, sems.at[1]),
    ]
    large = [
        pltpu.make_async_copy(
            weight.at[pl.ds(lower, chunk)], weight_out.at[pl.ds(lower, chunk)], sems.at[2 + index]
        )
        for index, lower in enumerate(range(0, weight.shape[0], chunk))
    ]
    for copy in large[:1] + small + large[1:]:
        copy.start()
    for index, copy in enumerate(large):
        copy.wait()
        if (index + 1) * chunk <= turned_out.shape[1]:
            turn(weight_out, turned_out, index * chunk, (index + 1) * chunk, 0)
    for copy in small:
        copy.wait()


def turn_kernel(weight, out, *, chunk):
    done = weight.shape[0] - out.shape[1]
    for lower in range(done, weight.shape[0], chunk):
        turn(weight, out, lower, lower + chunk, done)


def input_grad_kernel(other, own, first, second, send_out, keep_out, *, tile):
    rows = own.shape[0] // 2
    core = lax.axis_index("col") % 2
    mine = pl.multiple_of(core * rows, rows)
    theirs = pl.multiple_of((1 - core) * rows, rows)
    grads = jnp.concatenate(
        [ref[pl.ds(start, rows), :] for start in (theirs, mine) for ref in (other, own)], axis=0
    )
    offset = 0
    for turned in (first, second):
        for lower in range(0, turned.shape[1], tile):
            total = jnp.dot(grads, turned[:, lower : lower + tile], preferred_element_type=F32)
            columns = pl.ds(offset + lower, tile)
            send_out[:, columns] = total[: 2 * rows].astype(BF16)
            keep_out[:, columns] = total[2 * rows :]
        offset += turned.shape[1]


def pair_kernel(keep, received, *outs):
    rows = keep.shape[0] // 2
    matches = lax.axis_index("col") // 2 == lax.axis_index("row")
    straight = pl.multiple_of(jnp.where(matches, rows, 0), rows)
    crossing = pl.multiple_of(rows - straight, rows)
    for index, start in enumerate((crossing, straight)):
        total = (
            keep[pl.ds(start, rows), :] + received[pl.ds(start, rows), :].astype(F32)
        ).astype(BF16)
        for out in outs[index::2]:
            out[...] = total


def weight_grad_kernel(tokens, other, own, out, turned, blocks, sems, *, tile):
    turned[...] = tokens[...].T
    copies = []
    for index in range(out.shape[1] // tile):
        lower = index * tile
        grads = jnp.concatenate(
            [other[:, lower : lower + tile], own[:, lower : lower + tile]], axis=0
        )
        rows = out.shape[0] // 2
        for part in range(2):
            tall = pl.ds(part * rows, rows)
            blocks[index, tall, :] = jnp.dot(
                turned[tall, :], grads, preferred_element_type=F32
            ).astype(BF16)
            copy = pltpu.make_async_copy(
                blocks.at[index, pl.ds(part * rows, rows)],
                out.at[pl.ds(part * rows, rows), pl.ds(lower, tile)],
                sems.at[2 * index + part],
            )
            copy.start(priority=part)
            copies.append(copy)
    for copy in copies:
        copy.wait()


def hidden_kernel(keep, received, out):
    out[...] = (keep[...].astype(F32) + received[...].astype(F32)).astype(BF16)


def sum_kernel(hidden, *refs):
    *received, hidden_out, passed_out, passed_held, sems = refs
    copies = [pltpu.make_async_copy(hidden, hidden_out, sems.at[0])]
    copies[0].start()
    sums = [
        received[index][...].astype(F32) + received[index + 1][...].astype(F32)
        for index in (0, 2)
    ]
    section = lax.axis_index("section")
    last = section == lax.axis_size("section") - 1
    passed = jnp.where(section % 2 == 0, sums[0], sums[1])
    passed_held[...] = jnp.where(last, jnp.zeros_like(passed), passed).astype(BF16)
    copies.append(pltpu.make_async_copy(passed_held, passed_out, sems.at[1]))
    copies[-1].start()
    for copy in copies:
        copy.wait()


def paired_step(tokens, weights, hidden_grads):
    own, weight, grads = tokens[0], weights[0], hidden_grads[0]
    rows, width = own.shape
    half, units = grads.shape
    grads_other = swapped(grads, "row", 1)
    across = swapped(own, "col", 2)
    beside = swapped(own, "col", 1)
    flops = 4 * half * width * units
    anywhere = pl.BlockSpec(memory_space=pltpu.HBM)
    chunk = 256
    early = chunk * 4
    weight, turned_first, own, grads = call(
        functools.partial(load_kernel, chunk=chunk),
        [
            jax.ShapeDtypeStruct(shape, BF16)
            for shape in (weight.shape, (units, early), own.shape, grads.shape)
        ],
        [pltpu.with_memory_space_constraint(value, pltpu.HBM) for value in (weight, own, grads)],
        scratch=[pltpu.SemaphoreType.DMA((2 + width // chunk,))],
        in_specs=[anywhere] * 3,
        moved=4 * width * units,
        limit=16 * MIB,
        name="load",
    )
    across, weight = lax.optimization_barrier((across, weight))
    diagonal = swapped(across, "col", 1)
    turned_second = call(
        functools.partial(turn_kernel, chunk=chunk),
        jax.ShapeDtypeStruct((units, width - early), BF16),
        (weight,),
        flops=2 * units * (width - early) * chunk,
        moved=4 * units * (width - early),
        name="turn",
    )
    diagonal, turned_second = lax.optimization_barrier((diagonal, turned_second))
    tokens_all, hidden_send, hidden_keep = call(
        functools.partial(forward_kernel, tile=512),
        [
            jax.ShapeDtypeStruct((4 * rows, width), BF16),
            jax.ShapeDtypeStruct((half, units), BF16),
            jax.ShapeDtypeStruct((half, units), BF16),
        ],
        (own, beside, across, diagonal, weight),
        flops=flops,
        moved=2 * width * units,
        name="forward",
    )
    hidden_received = swapped(hidden_send, "row", 1)
    piece_send, piece_keep = call(
        functools.partial(input_grad_kernel, tile=256),
        [
            jax.ShapeDtypeStruct((half, width), BF16),
            jax.ShapeDtypeStruct((half, width), F32),
        ],
        (grads_other, grads, turned_first, turned_second),
        flops=flops,
        moved=2 * width * units,
        name="input_grad",
    )
    piece_received = swapped(piece_send, "col", 1)
    pieces = call(
        pair_kernel,
        [jax.ShapeDtypeStruct((rows, width), BF16)] * 4,
        (piece_keep, piece_received),
        moved=8 * half * width,
        name="pair_sum",
    )
    tokens_late, *pieces = lax.optimization_barrier((tokens_all, *pieces))
    received = [
        paired_sections(piece, index // 2, index % 2 == 0) for index, piece in enumerate(pieces)
    ]
    block = 512
    weight_grad = call(
        functools.partial(weight_grad_kernel, tile=block),
        jax.ShapeDtypeStruct((width, units), BF16),
        (tokens_late, grads_other, grads),
        scratch=[
            pltpu.VMEM((width, 2 * half), BF16),
            pltpu.VMEM((units // block, width, block), BF16),
            pltpu.SemaphoreType.DMA((2 * units // block,)),
        ],
        out_specs=[anywhere],
        flops=flops,
        moved=2 * width * units,
        name="weight_grad",
    )
    hidden_received, weight_grad = lax.optimization_barrier((hidden_received, weight_grad))
    hidden = call(
        hidden_kernel,
        jax.ShapeDtypeStruct((half, units), BF16),
        (hidden_keep, hidden_received),
        moved=6 * half * units,
        name="hidden_sum",
    )
    hidden, passed_grad = call(
        sum_kernel,
        [jax.ShapeDtypeStruct((half, units), BF16), jax.ShapeDtypeStruct((rows, width), BF16)],
        [hidden] + received,
        scratch=[
            pltpu.VMEM((rows, width), BF16),
            pltpu.SemaphoreType.DMA((2,)),
        ],
        out_specs=[anywhere] * 2,
        moved=8 * half * units,
        name="final_sum",
    )
    return (hidden[None], weight_grad[None], passed_grad[None])


def solution(mesh):
    in_specs = (P("section", "col", "row"), P("section", "row", "col"), P("section", "row", "col"))
    out_specs = (P("section", "row", "col"), P("section", "row", "col"), P("section", "col", "row"))
    paired = mesh.shape["row"] == 2 and mesh.shape["col"] == 4
    return jax.shard_map(
        paired_step if paired else general_step,
        mesh=mesh,
        in_specs=in_specs,
        out_specs=out_specs,
        check_vma=False,
    )
```

```python
import functools

import jax
import jax.numpy as jnp
from jax import lax
from jax.experimental import pallas as pl
from jax.experimental.pallas import tpu as pltpu
from jax.sharding import PartitionSpec as P

F32 = jnp.float32
BF16 = jnp.bfloat16
VMEM = pl.BlockSpec(memory_space=pltpu.VMEM)
MIB = 1 << 20


def shifted(value, axis, steps):
    count = lax.axis_size(axis)
    leading, last = (max(0, -steps), min(count, count - steps))
    return lax.ppermute(value, axis, [(source, source + steps) for source in range(leading, last)])


def paired_sections(value, first, crossing):
    sections, columns = lax.axis_size("section"), lax.axis_size("col")
    pairs = []
    for section in range(sections):
        partner = section + 1 if (section - first) % 2 == 0 else section - 1
        for col in range(columns):
            if 0 <= partner < sections:
                target = (partner, col ^ 2 if crossing else col)
            else:
                target = (section, col ^ 1)
            pairs.append((section * columns + col, target[0] * columns + target[1]))
    return lax.ppermute(value, ("section", "col"), pairs)


def swapped(value, axis, distance):
    count = lax.axis_size(axis)
    return lax.ppermute(value, axis, [(source, source ^ distance) for source in range(count)])


def general_step(tokens, weights, hidden_grads):
    token_tile, weight_tile, grad_tile = tokens[0], weights[0], hidden_grads[0]
    tokens_all = lax.all_gather(token_tile, "col", axis=0, tiled=True)
    hidden_sum = lax.psum_scatter(
        jnp.dot(tokens_all, weight_tile, preferred_element_type=F32).astype(BF16),
        "row",
        scatter_dimension=0,
        tiled=True,
    )
    grad_piece = lax.all_gather(grad_tile, "row", axis=0, tiled=True)
    weight_grad = lax.dot_general(
        tokens_all, grad_piece, (((0,), (0,)), ((), ())), preferred_element_type=F32
    ).astype(BF16)
    input_piece = lax.dot_general(
        grad_piece, weight_tile, (((1,), (1,)), ((), ())), preferred_element_type=F32
    )
    input_grad = lax.psum_scatter(input_piece, "col", scatter_dimension=0, tiled=True).astype(BF16)
    return (hidden_sum[None], weight_grad[None], shifted(input_grad, "section", -1)[None])


def call(kernel, out_shapes, args, scratch=(), flops=0, moved=0, name=None, grid=(), in_specs=None, out_specs=None, limit=16 * MIB, aliases={}):
    single = not isinstance(out_shapes, (list, tuple))
    shapes = [out_shapes] if single else list(out_shapes)
    in_specs = in_specs or [VMEM] * len(args)
    out_specs = out_specs or [VMEM] * len(shapes)
    result = pl.pallas_call(
        kernel,
        grid=grid,
        out_shape=shapes,
        in_specs=in_specs,
        out_specs=out_specs,
        scratch_shapes=list(scratch),
        input_output_aliases=aliases,
        compiler_params=pltpu.CompilerParams(vmem_limit_bytes=limit),
        cost_estimate=pl.CostEstimate(flops=flops, bytes_accessed=moved, transcendentals=0),
        name=name,
    )(*args)
    return result[0] if single else result


def forward_kernel(own, beside, across, diagonal, weight, tokens_out, send_out, keep_out, *, tile):
    rows = own.shape[0]
    row, col = lax.axis_index("row"), lax.axis_index("col")
    chip, core = col // 2, col % 2
    near = jnp.where(chip == row, 2 * rows, 0)
    far = 2 * rows - near
    for ref, start in (
        (own, near + core * rows),
        (beside, near + (1 - core) * rows),
        (across, far + core * rows),
        (diagonal, far + (1 - core) * rows),
    ):
        tokens_out[pl.ds(pl.multiple_of(start, rows), rows), :] = ref[...]
    half = 2 * rows
    for lower in range(0, weight.shape[1], tile):
        product = jnp.dot(
            tokens_out[...], weight[:, lower : lower + tile], preferred_element_type=F32
        ).astype(BF16)
        send_out[:, lower : lower + tile] = product[:half]
        keep_out[:, lower : lower + tile] = product[half:]


def turn(weight, out, lower, upper, offset):
    size = min(256, weight.shape[1])
    down = lax.broadcasted_iota(jnp.int32, (size, size), 0)
    right = lax.broadcasted_iota(jnp.int32, (size, size), 1)
    identity = jnp.where(down == right, 1.0, 0.0).astype(BF16)
    for unit in range(0, weight.shape[1], size):
        out[unit : unit + size, lower - offset : upper - offset] = lax.dot_general(
            identity,
            weight[lower:upper, unit : unit + size],
            (((1,), (1,)), ((), ())),
            preferred_element_type=F32,
        ).astype(BF16)


def load_kernel(weight, own, grads, weight_out, turned_out, own_out, grads_out, sems, *, chunk):
    small = [
        pltpu.make_async_copy(own, own_out, sems.at[0]),
        pltpu.make_async_copy(grads, grads_out, sems.at[1]),
    ]
    large = [
        pltpu.make_async_copy(
            weight.at[pl.ds(lower, chunk)], weight_out.at[pl.ds(lower, chunk)], sems.at[2 + index]
        )
        for index, lower in enumerate(range(0, weight.shape[0], chunk))
    ]
    for copy in large[:1] + small + large[1:]:
        copy.start()
    for index, copy in enumerate(large):
        copy.wait()
        if (index + 1) * chunk <= turned_out.shape[1]:
            turn(weight_out, turned_out, index * chunk, (index + 1) * chunk, 0)
    for copy in small:
        copy.wait()


def turn_kernel(weight, out, *, chunk):
    done = weight.shape[0] - out.shape[1]
    for lower in range(done, weight.shape[0], chunk):
        turn(weight, out, lower, lower + chunk, done)


def input_grad_kernel(other, own, first, second, send_out, keep_out, *, tile):
    rows = own.shape[0] // 2
    core = lax.axis_index("col") % 2
    mine = pl.multiple_of(core * rows, rows)
    theirs = pl.multiple_of((1 - core) * rows, rows)
    grads = jnp.concatenate(
        [ref[pl.ds(start, rows), :] for start in (theirs, mine) for ref in (other, own)], axis=0
    )
    offset = 0
    for turned in (first, second):
        for lower in range(0, turned.shape[1], tile):
            total = jnp.dot(grads, turned[:, lower : lower + tile], preferred_element_type=F32)
            columns = pl.ds(offset + lower, tile)
            send_out[:, columns] = total[: 2 * rows].astype(BF16)
            keep_out[:, columns] = total[2 * rows :]
        offset += turned.shape[1]


def pair_kernel(keep, received, *outs):
    rows = keep.shape[0] // 2
    matches = lax.axis_index("col") // 2 == lax.axis_index("row")
    straight = pl.multiple_of(jnp.where(matches, rows, 0), rows)
    crossing = pl.multiple_of(rows - straight, rows)
    for start, chosen in ((straight, (0, 3)), (crossing, (1, 2))):
        total = (
            keep[pl.ds(start, rows), :] + received[pl.ds(start, rows), :].astype(F32)
        ).astype(BF16)
        for index in chosen:
            outs[index][...] = total


def weight_grad_kernel(tokens, other, own, out, turned, blocks, sems, *, tile):
    turned[...] = tokens[...].T
    copies = []
    for index in range(out.shape[1] // tile):
        lower = index * tile
        grads = jnp.concatenate(
            [other[:, lower : lower + tile], own[:, lower : lower + tile]], axis=0
        )
        rows = out.shape[0] // 2
        for part in range(2):
            tall = pl.ds(part * rows, rows)
            blocks[index, tall, :] = jnp.dot(
                turned[tall, :], grads, preferred_element_type=F32
            ).astype(BF16)
            copy = pltpu.make_async_copy(
                blocks.at[index, pl.ds(part * rows, rows)],
                out.at[pl.ds(part * rows, rows), pl.ds(lower, tile)],
                sems.at[2 * index + part],
            )
            copy.start(priority=part)
            copies.append(copy)
    for copy in copies:
        copy.wait()


def hidden_kernel(keep, received, out):
    out[...] = (keep[...].astype(F32) + received[...].astype(F32)).astype(BF16)


def sum_kernel(hidden, *refs):
    *received, hidden_out, passed_out, passed_held, sems = refs
    copies = [pltpu.make_async_copy(hidden, hidden_out, sems.at[0])]
    copies[0].start()
    sums = [
        received[index][...].astype(F32) + received[index + 1][...].astype(F32)
        for index in (0, 2)
    ]
    section = lax.axis_index("section")
    last = section == lax.axis_size("section") - 1
    passed = jnp.where(section % 2 == 0, sums[0], sums[1])
    passed_held[...] = jnp.where(last, jnp.zeros_like(passed), passed).astype(BF16)
    copies.append(pltpu.make_async_copy(passed_held, passed_out, sems.at[1]))
    copies[-1].start()
    for copy in copies:
        copy.wait()


def paired_step(tokens, weights, hidden_grads):
    own, weight, grads = tokens[0], weights[0], hidden_grads[0]
    rows, width = own.shape
    half, units = grads.shape
    grads_other = swapped(grads, "row", 1)
    across = swapped(own, "col", 2)
    beside = swapped(own, "col", 1)
    flops = 4 * half * width * units
    anywhere = pl.BlockSpec(memory_space=pltpu.HBM)
    chunk = 256
    early = chunk * 4
    weight, turned_first, own, grads = call(
        functools.partial(load_kernel, chunk=chunk),
        [
            jax.ShapeDtypeStruct(shape, BF16)
            for shape in (weight.shape, (units, early), own.shape, grads.shape)
        ],
        [pltpu.with_memory_space_constraint(value, pltpu.HBM) for value in (weight, own, grads)],
        scratch=[pltpu.SemaphoreType.DMA((2 + width // chunk,))],
        in_specs=[anywhere] * 3,
        moved=4 * width * units,
        limit=16 * MIB,
        name="load",
    )
    across, weight = lax.optimization_barrier((across, weight))
    diagonal = swapped(across, "col", 1)
    turned_second = call(
        functools.partial(turn_kernel, chunk=chunk),
        jax.ShapeDtypeStruct((units, width - early), BF16),
        (weight,),
        flops=2 * units * (width - early) * chunk,
        moved=4 * units * (width - early),
        name="turn",
    )
    diagonal, turned_second = lax.optimization_barrier((diagonal, turned_second))
    tokens_all, hidden_send, hidden_keep = call(
        functools.partial(forward_kernel, tile=512),
        [
            jax.ShapeDtypeStruct((4 * rows, width), BF16),
            jax.ShapeDtypeStruct((half, units), BF16),
            jax.ShapeDtypeStruct((half, units), BF16),
        ],
        (own, beside, across, diagonal, weight),
        flops=flops,
        moved=2 * width * units,
        name="forward",
    )
    hidden_received = swapped(hidden_send, "row", 1)
    piece_send, piece_keep = call(
        functools.partial(input_grad_kernel, tile=256),
        [
            jax.ShapeDtypeStruct((half, width), BF16),
            jax.ShapeDtypeStruct((half, width), F32),
        ],
        (grads_other, grads, turned_first, turned_second),
        flops=flops,
        moved=2 * width * units,
        name="input_grad",
    )
    piece_received = swapped(piece_send, "col", 1)
    pieces = call(
        pair_kernel,
        [jax.ShapeDtypeStruct((rows, width), BF16)] * 4,
        (piece_keep, piece_received),
        moved=8 * half * width,
        name="pair_sum",
    )
    tokens_late, *pieces = lax.optimization_barrier((tokens_all, *pieces))
    received = [
        paired_sections(piece, index // 2, index in (1, 2)) for index, piece in enumerate(pieces)
    ]
    block = 512
    weight_grad = call(
        functools.partial(weight_grad_kernel, tile=block),
        jax.ShapeDtypeStruct((width, units), BF16),
        (tokens_late, grads_other, grads),
        scratch=[
            pltpu.VMEM((width, 2 * half), BF16),
            pltpu.VMEM((units // block, width, block), BF16),
            pltpu.SemaphoreType.DMA((2 * units // block,)),
        ],
        out_specs=[anywhere],
        flops=flops,
        moved=2 * width * units,
        name="weight_grad",
    )
    hidden_received, weight_grad = lax.optimization_barrier((hidden_received, weight_grad))
    hidden = call(
        hidden_kernel,
        jax.ShapeDtypeStruct((half, units), BF16),
        (hidden_keep, hidden_received),
        moved=6 * half * units,
        name="hidden_sum",
    )
    hidden, passed_grad = call(
        sum_kernel,
        [jax.ShapeDtypeStruct((half, units), BF16), jax.ShapeDtypeStruct((rows, width), BF16)],
        [hidden] + received,
        scratch=[
            pltpu.VMEM((rows, width), BF16),
            pltpu.SemaphoreType.DMA((2,)),
        ],
        out_specs=[anywhere] * 2,
        moved=8 * half * units,
        name="final_sum",
    )
    return (hidden[None], weight_grad[None], passed_grad[None])


def solution(mesh):
    in_specs = (P("section", "col", "row"), P("section", "row", "col"), P("section", "row", "col"))
    out_specs = (P("section", "row", "col"), P("section", "row", "col"), P("section", "col", "row"))
    paired = mesh.shape["row"] == 2 and mesh.shape["col"] == 4
    return jax.shard_map(
        paired_step if paired else general_step,
        mesh=mesh,
        in_specs=in_specs,
        out_specs=out_specs,
        check_vma=False,
    )
```
